128 devices in a mesh: sec: 4 (over y), col: 32 (over z, x, core).
Axes of the slice: x: 4, y: 4, z: 4, core: 2. Of those that a mesh axis runs over, the one named last changes fastest.
Arguments:
- column_state: float32 [4, 163840, 128], P('sec', 'col'), may hold values from -6 to 6
- mixing: float32 [4, 163840, 128], P('sec', 'col'), may hold values from 0.05 to 20
- surface_mask: int32 [4, 256, 128], P('sec', 'col'), may hold values 0 or 1
- pairings: int32 [4, 1728, 3], P('sec', 'col'), may hold values from 0 to 1023, as said below
- pairing_count: int32 [4, 32], P('sec', 'col'), may hold values from 3 to 54, as said below
- remap_weights: float32 [4, 65536, 128], P('sec', 'col'), may hold values from -0.5 to 0.5
Outputs:
- new_state: float32 [4, 163840, 128], P('sec', 'col')
The draws below stay inside these ranges and needn't reach their ends.
Inputs may be any that keep to these rules, and one draw needn't show every extreme that they name: `pairings`: entry e of device d's list is used when e < pairing_count of d; used entries come first. Column 0 is a block of d, column 2 a weight block of d (below 16), column 1 a global block of the other component (ocean blocks for atmosphere devices, atmosphere blocks for ocean devices) on a device whose col differs from d's by -1, 0 or 1 cyclically. At most 6 used entries of one device name blocks of any one device. `pairing_count`: atmosphere devices use at most 18 entries.
All inputs are finite; a program needn't handle non-finite values. No bound on the sum of `surface_mask` on one device may be relied on, other than what follows from the above.
Results may differ from the reference program's by a relative error of at most 0.0003.
Values sent between devices are 32-bit elements; how exact they have to be, the bound alone decides.
No kernel may reach another device: no remote copies, remote signals or barrier semaphores. Data moves between devices by JAX's collectives and lax.ppermute only.
A program may use at most 192 MiB of HBM per device.

```python
import math
import jax
import jax.numpy as jnp
from jax import lax

CELLS = 128
LEV_ATM = 128
LEV_OCN = 80
TRC_ATM = 5
TRC_OCN = 8
COUPLED = 4
BLK_DEV = 8
CAP = 6
WBLK = 16
SUBSTEPS = 2
OVL = 54
ROWS_DEV = 5120
NBLK = 1024
N_SEC = 4
N_COL = 32


def pairing_tables(key):
    device_total = N_SEC * N_COL
    pair_total = 3 * (N_SEC - 1)
    slot_total = pair_total * CAP
    device_ids = jnp.arange(device_total, dtype=jnp.int32)
    device_sec = device_ids // N_COL
    device_col = device_ids % N_COL
    ocean_rows = device_sec == N_SEC - 1
    pair_index = jnp.arange(pair_total, dtype=jnp.int32)
    col_shift = pair_index % 3 - 1
    peer_col = (device_col[:, None] + col_shift[None, :]) % N_COL
    peer_sec = jnp.where(ocean_rows[:, None], pair_index[None, :] // 3, N_SEC - 1)
    allowed = ocean_rows[:, None] | (pair_index[None, :] < 3)
    focus_col = jax.random.randint(jax.random.fold_in(key, 11), (), 0, N_COL)
    pair_sizes = jax.random.randint(jax.random.fold_in(key, 12), (device_total, pair_total), 1, CAP + 1)
    forced = (device_col[:, None] == focus_col) | (peer_col == focus_col)
    pair_sizes = jnp.where(forced, CAP, pair_sizes)
    pair_sizes = jnp.where(allowed, pair_sizes, 0)
    slot_index = jnp.arange(slot_total, dtype=jnp.int32)
    slot_pair = slot_index // CAP
    slot_rank = slot_index % CAP
    in_use = slot_rank[None, :] < pair_sizes[:, slot_pair]
    scores = jax.random.randint(jax.random.fold_in(key, 13), (device_total, slot_total), 0, 65536)
    scores = jnp.where(in_use, scores, scores + 65536) * slot_total + slot_index[None, :]
    ordering = jnp.argsort(scores, axis=1).astype(jnp.int32)
    entry_pair = ordering // CAP
    target_sec = jnp.take_along_axis(peer_sec, entry_pair, axis=1)
    target_col = jnp.take_along_axis(peer_col, entry_pair, axis=1)
    local_block = jax.random.randint(jax.random.fold_in(key, 14), (device_total, slot_total), 0, BLK_DEV)
    target_block = (target_sec * N_COL + target_col) * BLK_DEV + local_block
    source_block = jax.random.randint(jax.random.fold_in(key, 15), (device_total, slot_total), 0, BLK_DEV)
    weight_block = jax.random.randint(jax.random.fold_in(key, 16), (device_total, slot_total), 0, WBLK)
    listing = jnp.stack([source_block, target_block, weight_block], axis=-1).astype(jnp.int32)
    totals = jnp.sum(pair_sizes, axis=1).astype(jnp.int32)
    return (listing.reshape(N_SEC, N_COL * slot_total, 3), totals.reshape(N_SEC, N_COL))


def draw_pairings(key, part):
    return pairing_tables(key)[0]


def draw_pairing_count(key, part):
    return pairing_tables(key)[1]


def with_ends(result, own_key, smallest, high):
    longest = result.shape.index(max(result.shape))
    spots = []
    for shift in (0, 1):
        where = [jax.random.randint(jax.random.fold_in(own_key, axis), (), 0, length) for axis, length in enumerate(result.shape)]
        where[longest] = (where[longest] + shift) % result.shape[longest]
        spots.append(tuple(where))
    return result.at[spots[0]].set(smallest).at[spots[1]].set(high)


def shard_levels(own_key, extent, pieces, low, largest):
    level, own = 1.0, jax.random.fold_in(own_key, 6)
    for position, parts in pieces:
        draws = jnp.exp(jax.random.uniform(jax.random.fold_in(own, position), (parts,), jnp.float32, low / len(pieces), largest / len(pieces)))
        level = level * jnp.repeat(draws, extent[position] // parts).reshape([-1 if axis == position else 1 for axis in range(len(extent))])
    return level


def normal_values(key, dims, scale, most, pieces=(), kind=jnp.bfloat16):
    gain = shard_levels(key, dims, pieces, -0.22, 0.18) if pieces else 1.0
    array = jax.random.normal(key, dims, jnp.float32) * scale * gain
    return jnp.minimum(jnp.maximum(array, -most), most).astype(kind)


def setup_inputs(seed: int = 0) -> dict:
    streams_of = jax.random.split(jax.random.key(seed), 7)
    column_state = normal_values(streams_of[0], (N_SEC, N_COL * ROWS_DEV, CELLS), 1.0, 6.0, ((0, 4), (1, 32)), jnp.float32)
    mixing = jnp.clip(jnp.exp(math.log(20.0) - 5.9914645 * jax.random.uniform(streams_of[1], (N_SEC, N_COL * ROWS_DEV, CELLS), jnp.float32) ** shard_levels(streams_of[1], (N_SEC, N_COL * ROWS_DEV, CELLS), ((0, 4), (1, 32)), -0.2, 0.2)), 0.05, 20.0)
    surface_mask = with_ends((jax.random.randint(streams_of[2], (N_SEC, N_COL * BLK_DEV, CELLS), 0, 4) < 3).astype(jnp.int32), jax.random.fold_in(streams_of[2], 1), 0, 1)
    pairings = draw_pairings(jax.random.fold_in(streams_of[6], 71), 0)
    pairing_count = draw_pairing_count(jax.random.fold_in(streams_of[6], 71), 0)
    remap_weights = normal_values(streams_of[5], (N_SEC, N_COL * WBLK * CELLS, CELLS), CELLS ** -0.5, 0.5, ((0, 4), (1, 32)), jnp.float32)
    return dict(column_state=column_state, mixing=mixing, surface_mask=surface_mask, pairings=pairings, pairing_count=pairing_count, remap_weights=remap_weights)


highest = lax.Precision.HIGHEST


def tridiagonal(right_side, coupling, interface):
    shifted = jnp.concatenate([jnp.zeros_like(coupling[:1]), coupling[:-1]], axis=0)
    diagonal = 1.0 + shifted + coupling
    deepest = right_side.shape[0] - 1
    right_side = right_side.at[deepest].add(coupling[deepest] * interface)

    def forward(carried, inputs):
        upper_prev, solved_prev = carried
        lower_band, diag_band, upper_band, source = inputs
        divisor = diag_band - lower_band * upper_prev
        upper_next = upper_band / divisor
        solved_next = (source - lower_band * solved_prev) / divisor
        return (upper_next, solved_next), (upper_next, solved_next)

    initial = (jnp.zeros_like(interface), jnp.zeros_like(interface))
    _, (uppers, partial_values) = lax.scan(forward, initial, (-shifted, diagonal, -coupling, right_side))

    def backward(following, inputs):
        upper_band, partial_value = inputs
        current = partial_value - upper_band * following
        return current, current

    _, solved = lax.scan(backward, jnp.zeros_like(interface), (uppers, partial_values), reverse=True)
    return solved


def remap(values, listing, used_count, weights):
    def one_device(operands):
        surface_vals, table_rows, count_here, weight_rows = operands
        entries = jnp.einsum('enc,ecd->end', surface_vals[table_rows[:, 0]], weight_rows[table_rows[:, 2]], precision=highest)
        in_use = jnp.arange(OVL, dtype=jnp.int32) < count_here
        target = jnp.where(in_use, table_rows[:, 1], NBLK).astype(jnp.int32)
        return entries, target

    entries, target = lax.map(one_device, (values, listing, used_count, weights))
    summed = jnp.zeros((NBLK, COUPLED, CELLS), jnp.float32)
    return summed.at[target.reshape(-1)].add(entries.reshape(-1, COUPLED, CELLS), mode="drop")


def reference(column_state, mixing, surface_mask, pairings, pairing_count, remap_weights):
    devices_all = N_SEC * N_COL
    listing = pairings.reshape(devices_all, OVL, 3)
    used_count = pairing_count.reshape(devices_all)
    weights = remap_weights.reshape(devices_all, WBLK, CELLS, CELLS)
    surface = surface_mask.astype(jnp.float32).reshape(N_SEC, N_COL, BLK_DEV, CELLS)
    shapes = [(LEV_ATM, TRC_ATM) if section < N_SEC - 1 else (LEV_OCN, TRC_OCN) for section in range(N_SEC)]
    profiles = []
    couplings = []
    for section in range(N_SEC):
        levels, tracers = shapes[section]
        profile = column_state[section].reshape(N_COL, levels, BLK_DEV, tracers, CELLS)
        coupling = mixing[section].reshape(N_COL, levels, BLK_DEV, tracers, CELLS)
        coupling = coupling.at[:, levels - 1].multiply(surface[section][:, :, None, :])
        profiles.append(jnp.moveaxis(profile, 1, 0).reshape(levels, N_COL * BLK_DEV * tracers, CELLS))
        couplings.append(jnp.moveaxis(coupling, 1, 0).reshape(levels, N_COL * BLK_DEV * tracers, CELLS))
    for substep in range(SUBSTEPS):
        values = []
        for section in range(N_SEC):
            levels, tracers = shapes[section]
            bottom = profiles[section][levels - 1].reshape(N_COL, BLK_DEV, tracers, CELLS)[:, :, :COUPLED]
            values.append(bottom * surface[section][:, :, None, :])
        values = jnp.stack(values).reshape(devices_all, BLK_DEV, COUPLED, CELLS)
        boundary = remap(values, listing, used_count, weights).reshape(N_SEC, N_COL, BLK_DEV, COUPLED, CELLS)
        for section in range(N_SEC):
            levels, tracers = shapes[section]
            padding = jnp.zeros((N_COL, BLK_DEV, tracers - COUPLED, CELLS), jnp.float32)
            interface = jnp.concatenate([boundary[section], padding], axis=2).reshape(-1, CELLS)
            profiles[section] = tridiagonal(profiles[section], couplings[section], interface)
    outputs = []
    for section in range(N_SEC):
        levels, tracers = shapes[section]
        restored = jnp.moveaxis(profiles[section].reshape(levels, N_COL, BLK_DEV, tracers, CELLS), 0, 1)
        outputs.append(restored.reshape(N_COL * levels * BLK_DEV * tracers, CELLS))
    return jnp.stack(outputs)
```

```python
from functools import partial

import jax
import jax.numpy as jnp
from jax import lax
from jax.experimental import pallas as pl
from jax.experimental.pallas import tpu as pltpu
from jax.sharding import PartitionSpec as P

CELLS = 128
LEV_ATM = 128
LEV_OCN = 80
TRC_ATM = 5
TRC_OCN = 8
COUPLED = 4
BLK = 8
WBLK = 16
ROWS = 5120
WIDE = BLK * COUPLED
CHUNK = 320
CHUNKS = ROWS // CHUNK
SECS = 4
ROTATIONS = SECS - 1
SPAN = ROTATIONS * WIDE

f32 = jnp.float32
bf16 = jnp.bfloat16
MIB = 1 << 20

ATM = (LEV_ATM, TRC_ATM)
OCN = (LEV_OCN, TRC_OCN)


def vmem():
    return pl.BlockSpec(memory_space=pltpu.VMEM)


def smem():
    return pl.BlockSpec(memory_space=pltpu.SMEM)


def anywhere():
    return pl.BlockSpec(memory_space=pl.ANY)


def call(kernel, outs, in_specs, scratch, limit, flops, nbytes, out_specs=None):
    return pl.pallas_call(
        kernel,
        out_shape=[jax.ShapeDtypeStruct(shape, kind) for shape, kind in outs],
        in_specs=in_specs,
        out_specs=out_specs or [vmem()] * len(outs),
        scratch_shapes=scratch,
        compiler_params=pltpu.CompilerParams(vmem_limit_bytes=limit * MIB),
        cost_estimate=pl.CostEstimate(flops=flops, bytes_accessed=nbytes, transcendentals=0),
    )


def per_component(body):
    ocean = lax.axis_index("sec") == SECS - 1
    pl.when(ocean)(partial(body, *OCN))
    pl.when(jnp.logical_not(ocean))(partial(body, *ATM))


def compact(tracers, rows):
    return jnp.concatenate(
        [rows[b * tracers : b * tracers + COUPLED] for b in range(BLK)], axis=0
    )


def spread(tracers, values, target):
    for b in range(BLK):
        target[b * tracers : b * tracers + COUPLED] = values[b * COUPLED : (b + 1) * COUPLED]
        rest = tracers - COUPLED
        target[b * tracers + COUPLED : (b + 1) * tracers] = jnp.zeros((rest, CELLS), f32)


def by_field(mask, fields):
    return jnp.concatenate(
        [jnp.broadcast_to(mask[b : b + 1], (fields, CELLS)) for b in range(BLK)], axis=0
    )


def send_products(surface, high, low, listing, count, products, own, near, far):
    part_high = surface.astype(bf16)
    part_low = (surface - part_high.astype(f32)).astype(bf16)
    left = jnp.concatenate([part_high, part_low], axis=0)
    for w in range(WBLK):
        rows = slice(w * CELLS, (w + 1) * CELLS)
        both = jnp.dot(left, high[rows], preferred_element_type=f32) + jnp.dot(
            left, low[rows], preferred_element_type=f32
        )
        products[w * BLK : (w + 1) * BLK] = (both[:WIDE] + both[WIDE:]).reshape(
            BLK, COUPLED, CELLS
        )
    for target in (own, near, far):
        target[...] = jnp.zeros_like(target)
    sec = lax.axis_index("sec")
    col = lax.axis_index("col")
    columns = lax.axis_size("col")

    def entry(e, carry):
        source = listing[e, 0]
        goal = listing[e, 1]
        weight = listing[e, 2]
        block = lax.rem(goal, BLK)
        device = lax.div(goal, BLK)
        to_col = lax.rem(device, columns)
        to_sec = lax.div(device, columns)
        slot = lax.rem(to_sec - sec + (SECS - 1), SECS) * BLK + block
        piece = products[weight * BLK + lax.rem(source, BLK)]
        same = to_col == col
        beside = to_col == jnp.bitwise_xor(col, 1)

        @pl.when(same)
        def _():
            own[slot] += piece

        @pl.when(beside)
        def _():
            near[slot] += piece

        @pl.when(jnp.logical_not(jnp.logical_or(same, beside)))
        def _():
            far[slot] += piece

        return carry

    lax.fori_loop(0, count[0, 0], entry, 0)


def first_kernel(tail, mask, listing, count, weights, own, near, far, high, low, top, products):
    source_cell = mask[...].astype(f32)
    split = weights[...].astype(bf16)
    high[...] = split
    low[...] = (weights[...] - split.astype(f32)).astype(bf16)

    def component(levels, tracers):
        width = BLK * tracers
        top[...] = compact(tracers, tail[tail.shape[0] - width :])

    per_component(component)
    surface = top[...] * by_field(source_cell, COUPLED)
    send_products(surface, high, low, listing, count, products, own, near, far)


def middle_kernel(
    got1, got2, got3, c_tail, d_tail, mask, listing, count, high, low, boundary, own, near, far, top, products
):
    source_cell = mask[...].astype(f32)
    arrived = got1[...] + got2[...] + got3[...]
    boundary[...] = arrived

    def component(levels, tracers):
        width = BLK * tracers
        start = c_tail.shape[0] - width
        top[...] = compact(tracers, d_tail[start:]) + compact(tracers, c_tail[start:]) * arrived

    per_component(component)
    surface = top[...] * by_field(source_cell, COUPLED)
    send_products(surface, high, low, listing, count, products, own, near, far)


def eliminate_kernel(state, mixing, mask, c, d, w, e, s_buf, r_buf, sems):
    def copies(i):
        rows = pl.ds(pl.multiple_of(i * CHUNK, CHUNK), CHUNK)
        return (
            pltpu.make_async_copy(state.at[rows], s_buf.at[rows], sems.at[0, i]),
            pltpu.make_async_copy(mixing.at[rows], r_buf.at[rows], sems.at[1, i]),
        )

    for i in range(CHUNKS):
        for copy in copies(i):
            copy.start()
    source_cell = mask[...].astype(f32)

    def component(levels, tracers):
        width = BLK * tracers
        per_chunk = CHUNK // width

        def chunk(i, carry):
            for copy in copies(i):
                copy.wait()

            @pl.when(i == CHUNKS - 1)
            def _():
                r_buf[ROWS - width :] *= by_field(source_cell, tracers)

            r_above, c_above, d_above = carry
            for j in range(per_chunk):
                rows = pl.ds(pl.multiple_of(i * CHUNK + j * width, 8), width)
                r = r_buf[rows]
                inverse = 1.0 / (1.0 + r + r_above * (1.0 - c_above))
                lower = r_above * inverse
                c_above = r * inverse
                d_above = s_buf[rows] * inverse + lower * d_above
                w[rows] = inverse
                e[rows] = lower
                c[rows] = c_above
                d[rows] = d_above
                r_above = r
            return r_above, c_above, d_above

        zero = jnp.zeros((width, CELLS), f32)
        lax.fori_loop(0, CHUNKS, chunk, (zero, zero, zero))

    per_component(component)


def substitute_kernel(c, d, y, g):
    def component(levels, tracers):
        width = BLK * tracers
        per_chunk = CHUNK // width

        def chunk(i, carry):
            y_below, g_below = carry
            for j in range(per_chunk):
                rows = pl.ds(pl.multiple_of(ROWS - i * CHUNK - (j + 1) * width, 8), width)
                upper = c[rows]
                y_below = d[rows] + upper * y_below
                g_below = upper * g_below
                y[rows] = y_below
                g[rows] = g_below
            return y_below, g_below

        zero = jnp.zeros((width, CELLS), f32)
        lax.fori_loop(0, CHUNKS, chunk, (zero, jnp.ones_like(zero)))

    per_component(component)


def again_kernel(boundary, y, g, w, e, c, u, wide):
    def component(levels, tracers):
        width = BLK * tracers
        per_chunk = CHUNK // width
        spread(tracers, boundary[...], wide)

        def down(i, d_above):
            b = wide[:width]
            for j in range(per_chunk):
                rows = pl.ds(pl.multiple_of(i * CHUNK + j * width, 8), width)
                d_above = (y[rows] + b * g[rows]) * w[rows] + e[rows] * d_above
                u[rows] = d_above
            return d_above

        def up(i, below):
            for j in range(per_chunk):
                rows = pl.ds(pl.multiple_of(ROWS - i * CHUNK - (j + 1) * width, 8), width)
                below = u[rows] + c[rows] * below
                u[rows] = below
            return below

        zero = jnp.zeros((width, CELLS), f32)
        lax.fori_loop(0, CHUNKS, down, zero)
        lax.fori_loop(0, CHUNKS, up, zero)

    per_component(component)


def finish_kernel(got1, got2, got3, u, g, out, wide, buf, sems):
    arrived = got1[...] + got2[...] + got3[...]

    def copy(i):
        rows = pl.ds(pl.multiple_of(i * CHUNK, CHUNK), CHUNK)
        return pltpu.make_async_copy(buf.at[rows], out.at[rows], sems.at[i])

    def component(levels, tracers):
        width = BLK * tracers
        per_chunk = CHUNK // width
        spread(tracers, arrived, wide)

        def chunk(i, carry):
            b = wide[:width]
            for j in range(per_chunk):
                rows = pl.ds(pl.multiple_of(i * CHUNK + j * width, 8), width)
                buf[rows] = u[rows] + b * g[rows]
            copy(i).start()
            return carry

        lax.fori_loop(0, CHUNKS, chunk, 0)

    per_component(component)

    def finish(i, carry):
        copy(i).wait()
        return carry

    lax.fori_loop(0, CHUNKS, finish, 0)


def rotations(mesh_shape):
    secs, cols = mesh_shape
    every = [(s, c) for s in range(secs) for c in range(cols)]

    def table(move):
        result = []
        for s, c in every:
            to_s, to_c = move(s, c)
            result.append((s * cols + c, (to_s % secs) * cols + to_c % cols))
        return result

    near = table(lambda s, c: (s, c ^ 1))
    far = table(lambda s, c: (s, c + 1 if c % 2 else c - 1))
    turns = [table(lambda s, c, k=k: (s + k, c)) for k in range(1, secs)]
    return near, far, turns


AXES = ("sec", "col")


def exchange(own, near, far, tables):
    to_near, to_far, turns = tables
    from_far = lax.ppermute(far, AXES, to_far)
    from_near = lax.ppermute(near, AXES, to_near)
    total = own + from_near + from_far
    return [
        lax.ppermute(total[k * BLK : (k + 1) * BLK], AXES, turns[k]).reshape(WIDE, CELLS)
        for k in range(ROTATIONS)
    ]


def shards(column_state, mixing, surface_mask, pairings, pairing_count, remap_weights):
    tables = rotations((lax.axis_size("sec"), lax.axis_size("col")))
    state = column_state[0]
    rates = mixing[0]
    mask = surface_mask[0]
    listing = pairings[0]
    weights = remap_weights[0]
    full = (ROWS, CELLS)
    payload = ((ROTATIONS * BLK, COUPLED, CELLS), f32)
    half = ((WBLK * CELLS, CELLS), bf16)
    tail = 64
    products = pltpu.VMEM((WBLK * BLK, COUPLED, CELLS), f32)
    top = pltpu.VMEM((WIDE, CELLS), f32)
    wide = pltpu.VMEM((tail, CELLS), f32)
    last = pl.BlockSpec((tail, CELLS), lambda i: (ROWS // tail - 1, 0))

    def whole(shape):
        return pl.BlockSpec(shape, lambda i: (0,) * len(shape))

    own, near, far, high, low = pl.pallas_call(
        first_kernel,
        out_shape=[jax.ShapeDtypeStruct(*spec) for spec in (payload, payload, payload, half, half)],
        grid=(1,),
        in_specs=[last, whole(mask.shape), smem(), smem(), whole(weights.shape)],
        out_specs=[whole(payload[0])] * 3 + [whole(half[0])] * 2,
        scratch_shapes=[top, products],
        compiler_params=pltpu.CompilerParams(vmem_limit_bytes=8 * MIB),
    )(state, mask, listing, pairing_count, weights)

    c, d, w, e = call(
        eliminate_kernel,
        [(full, f32)] * 4,
        [anywhere(), anywhere(), vmem()],
        [pltpu.VMEM(full, f32), pltpu.VMEM(full, f32), pltpu.SemaphoreType.DMA((2, CHUNKS))],
        8,
        20 * ROWS * CELLS,
        6 * ROWS * CELLS * 4,
    )(state, rates, mask)
    y, g = call(
        substitute_kernel, [(full, f32)] * 2, [vmem()] * 2, [], 2, 4 * ROWS * CELLS, 4 * ROWS * CELLS * 4
    )(c, d)

    got = exchange(own, near, far, tables)

    boundary, own, near, far = pl.pallas_call(
        middle_kernel,
        out_shape=[jax.ShapeDtypeStruct(*spec) for spec in (((WIDE, CELLS), f32), payload, payload, payload)],
        grid=(1,),
        in_specs=[whole((WIDE, CELLS))] * 3
        + [last, last, whole(mask.shape), smem(), smem()]
        + [whole(half[0])] * 2,
        out_specs=[whole((WIDE, CELLS))] + [whole(payload[0])] * 3,
        scratch_shapes=[top, products],
        compiler_params=pltpu.CompilerParams(vmem_limit_bytes=8 * MIB),
    )(*got, c, d, mask, listing, pairing_count, high, low)

    (u,) = call(
        again_kernel,
        [(full, f32)],
        [vmem()] * 6,
        [wide],
        2,
        6 * ROWS * CELLS,
        9 * ROWS * CELLS * 4,
    )(boundary, y, g, w, e, c)

    got = exchange(own, near, far, tables)

    (out,) = call(
        finish_kernel,
        [(full, f32)],
        [vmem()] * 5,
        [wide, pltpu.VMEM(full, f32), pltpu.SemaphoreType.DMA((CHUNKS,))],
        5,
        2 * ROWS * CELLS,
        3 * ROWS * CELLS * 4,
        [anywhere()],
    )(*got, u, g)
    return out[None]


def solution(mesh):
    placed = (
        P("sec", "col", None),
        P("sec", "col", None),
        P("sec", "col", None),
        P("sec", "col", None),
        P("sec", "col"),
        P("sec", "col", None),
    )
    return jax.shard_map(
        shards, mesh=mesh, in_specs=placed, out_specs=P("sec", "col", None), check_vma=False
    )
```

```python
from functools import partial

import jax
import jax.numpy as jnp
from jax import lax
from jax.experimental import pallas as pl
from jax.experimental.pallas import tpu as pltpu
from jax.sharding import PartitionSpec as P

CELLS = 128
LEV_ATM = 128
LEV_OCN = 80
TRC_ATM = 5
TRC_OCN = 8
COUPLED = 4
BLK = 8
WBLK = 16
PAIRS = WBLK // 2
ROWS = 5120
WIDE = BLK * COUPLED
CHUNK = 320
CHUNKS = ROWS // CHUNK
FETCH = 640
FETCHES = ROWS // FETCH
TAIL = 64
SECS = 4
ROTATIONS = SECS - 1
GOALS = 80

f32 = jnp.float32
bf16 = jnp.bfloat16
MIB = 1 << 20

ATM = (LEV_ATM, TRC_ATM)
OCN = (LEV_OCN, TRC_OCN)
AXES = ("sec", "col")


def call(kernel, outs, operands, in_hbm, scratch, limit, flops, nbytes, out_hbm=False, in_smem=0):
    vmem = pl.BlockSpec(memory_space=pltpu.VMEM)
    smem = pl.BlockSpec(memory_space=pltpu.SMEM)
    hbm = pl.BlockSpec(memory_space=pltpu.HBM)
    held = [pltpu.with_memory_space_constraint(x, pltpu.HBM) for x in operands[:in_hbm]]
    return pl.pallas_call(
        kernel,
        out_shape=[jax.ShapeDtypeStruct(shape, kind) for shape, kind in outs],
        in_specs=[hbm] * in_hbm + [vmem] * (len(operands) - in_hbm - in_smem) + [smem] * in_smem,
        out_specs=[hbm if out_hbm else vmem] * len(outs),
        scratch_shapes=scratch,
        compiler_params=pltpu.CompilerParams(vmem_limit_bytes=limit * MIB),
        cost_estimate=pl.CostEstimate(flops=flops, bytes_accessed=nbytes, transcendentals=0),
    )(*held, *operands[in_hbm:])


def per_component(body):
    ocean = lax.axis_index("sec") == SECS - 1
    pl.when(ocean)(partial(body, *OCN))
    pl.when(jnp.logical_not(ocean))(partial(body, *ATM))


def blocks_of(start, field, tracers):
    return pl.ds(start + field, BLK, stride=tracers)


def split(values):
    high = values.astype(bf16)
    return high, (values - high.astype(f32)).astype(bf16)


def doubled(surface):
    high, low = split(surface)
    return jnp.concatenate(
        [jnp.concatenate([high, high], axis=1), jnp.concatenate([low, low], axis=1)], axis=0
    )


def multiply(left, stacked, products, pair):
    both = jnp.dot(left, stacked, preferred_element_type=f32)
    both = both[:WIDE] + both[WIDE:]
    for half in range(2):
        for field in range(COUPLED):
            products[field, pl.ds((2 * pair + half) * BLK, BLK)] = both[
                field * BLK : (field + 1) * BLK, half * CELLS : (half + 1) * CELLS
            ]


def deliver(counts, products, targets):
    for first in range(0, COUPLED, 2):
        parts = [split(products[field]) for field in (first, first + 1)]
        right = jnp.concatenate(
            [jnp.concatenate([high, low], axis=0) for high, low in parts], axis=1
        )
        sums = jnp.dot(counts, right, preferred_element_type=f32)
        for t, target in enumerate(targets):
            for slot in range(ROTATIONS):
                row = (t * ROTATIONS + slot) * BLK
                for j in range(2):
                    target[slot * COUPLED + first + j] = sums[
                        row : row + BLK, j * CELLS : (j + 1) * CELLS
                    ]


def count_entries(listing, used):
    columns = lax.axis_size("col")
    sec = lax.axis_index("sec")
    col = lax.axis_index("col")
    source, goal, weight = listing[0], listing[1], listing[2]
    entries = goal.shape[1]
    device = lax.shift_right_logical(goal, BLK.bit_length() - 1)
    to_col = jnp.bitwise_and(device, columns - 1)
    to_sec = lax.shift_right_logical(device, columns.bit_length() - 1)
    slot = jnp.bitwise_and(to_sec - sec + (SECS - 1), SECS - 1)
    place = jnp.where(to_col == col, 0, jnp.where(to_col == jnp.bitwise_xor(col, 1), 1, 2))
    row = (place * ROTATIONS + slot) * BLK + jnp.bitwise_and(goal, BLK - 1)
    position = lax.broadcasted_iota(jnp.int32, (1, entries), 1)
    row = jnp.where(position < used, row, -1)
    combination = weight * BLK + jnp.bitwise_and(source, BLK - 1)
    goals = lax.broadcasted_iota(jnp.int32, (GOALS, entries), 0) == row
    combinations = lax.broadcasted_iota(jnp.int32, (WBLK * BLK, entries), 0) == combination
    counts = lax.dot_general(
        goals.astype(f32).astype(bf16),
        combinations.astype(f32).astype(bf16),
        (((1,), (1,)), ((), ())),
        preferred_element_type=f32,
    ).astype(bf16)
    return jnp.concatenate([counts, counts], axis=1)


def first_kernel(
    state, mask, listing, weights, count, own, near, far, stacked, counts, sea,
    tail, mask_buf, list_buf, w_buf, surface, products, sems, w_sems,
):
    small = [
        pltpu.make_async_copy(listing, list_buf, sems.at[0]),
        pltpu.make_async_copy(state.at[pl.ds(ROWS - TAIL, TAIL)], tail, sems.at[1]),
        pltpu.make_async_copy(mask, mask_buf, sems.at[2]),
    ]
    for copy in small:
        copy.start()

    def fetch(p):
        rows = pl.ds(p * 2 * CELLS, 2 * CELLS)
        return pltpu.make_async_copy(weights.at[rows], w_buf.at[rows], w_sems.at[p])

    for p in range(PAIRS):
        fetch(p).start()
    for copy in small:
        copy.wait()
    counts[...] = count_entries(list_buf[...], count[0, 0])
    cells = mask_buf[...].astype(f32)
    sea[...] = cells

    def component(levels, tracers):
        for field in range(COUPLED):
            surface[field * BLK : (field + 1) * BLK] = (
                tail[blocks_of(TAIL - BLK * tracers, field, tracers)] * cells
            )

    per_component(component)
    left = doubled(surface[...])
    for p in range(PAIRS):
        fetch(p).wait()
        base = p * 2 * CELLS
        high0, low0 = split(w_buf[base : base + CELLS])
        high1, low1 = split(w_buf[base + CELLS : base + 2 * CELLS])
        both = jnp.concatenate(
            [jnp.concatenate([high0, high1], axis=1), jnp.concatenate([low0, low1], axis=1)], axis=0
        )
        stacked[base : base + 2 * CELLS] = both
        multiply(left, both, products, p)
    deliver(counts[...], products, (own, near, far))


def middle_kernel(
    got1, got2, got3, y_top, g_top, sea, stacked, counts, boundary, own, near, far, surface, products
):
    for field in range(COUPLED):
        arrived = got1[field] + got2[field] + got3[field]
        boundary[field] = arrived
        surface[field * BLK : (field + 1) * BLK] = (
            y_top[field] + g_top[field] * arrived
        ) * sea[...]
    left = doubled(surface[...])
    for p in range(PAIRS):
        base = p * 2 * CELLS
        multiply(left, stacked[base : base + 2 * CELLS], products, p)
    deliver(counts[...], products, (own, near, far))


def sweep_kernel(state, mixing, sea, c, w, e, y, g, y_top, g_top, s_buf, r_buf, d, sems):
    def copies(i):
        rows = pl.ds(pl.multiple_of(i * FETCH, FETCH), FETCH)
        return (
            pltpu.make_async_copy(state.at[rows], s_buf.at[rows], sems.at[0, i]),
            pltpu.make_async_copy(mixing.at[rows], r_buf.at[rows], sems.at[1, i]),
        )

    for i in range(FETCHES):
        for copy in copies(i):
            copy.start()

    def component(levels, tracers):
        width = BLK * tracers
        zero = jnp.zeros((width, CELLS), f32)

        def eliminate(i, carry):
            @pl.when(lax.rem(i, FETCH // CHUNK) == 0)
            def _():
                for copy in copies(lax.div(i, FETCH // CHUNK)):
                    copy.wait()

            @pl.when(i == CHUNKS - 1)
            def _():
                for field in range(tracers):
                    r_buf[blocks_of(ROWS - width, field, tracers)] *= sea[...]

            r_above, c_above, d_above = carry
            for j in range(CHUNK // width):
                rows = pl.ds(pl.multiple_of(i * CHUNK + j * width, 8), width)
                r = r_buf[rows]
                inverse = 1.0 / (1.0 + r + r_above * (1.0 - c_above))
                lower = r_above * inverse
                c_above = r * inverse
                d_above = s_buf[rows] * inverse + lower * d_above
                w[rows] = inverse
                e[rows] = lower
                c[rows] = c_above
                d[rows] = d_above
                r_above = r
            return r_above, c_above, d_above

        lax.fori_loop(0, CHUNKS, eliminate, (zero, zero, zero))
        for field in range(COUPLED):
            rows = blocks_of(ROWS - width, field, tracers)
            y_top[field] = d[rows]
            g_top[field] = c[rows]

        def substitute(i, carry):
            y_below, g_below = carry
            for j in range(CHUNK // width):
                rows = pl.ds(pl.multiple_of(ROWS - i * CHUNK - (j + 1) * width, 8), width)
                upper = c[rows]
                y_below = d[rows] + upper * y_below
                g_below = upper * g_below
                y[rows] = y_below
                g[rows] = g_below
            return y_below, g_below

        lax.fori_loop(0, CHUNKS, substitute, (zero, jnp.ones_like(zero)))

    per_component(component)


def spread(values, tracers, wide):
    wide[...] = jnp.zeros_like(wide)
    for field in range(COUPLED):
        wide[blocks_of(0, field, tracers)] = values[field]


def again_kernel(boundary, y, g, w, e, c, u, wide):
    def component(levels, tracers):
        width = BLK * tracers
        spread(boundary, tracers, wide)
        zero = jnp.zeros((width, CELLS), f32)

        def down(i, above):
            b = wide[:width]
            for j in range(CHUNK // width):
                rows = pl.ds(pl.multiple_of(i * CHUNK + j * width, 8), width)
                above = (y[rows] + b * g[rows]) * w[rows] + e[rows] * above
                u[rows] = above
            return above

        def up(i, below):
            for j in range(CHUNK // width):
                rows = pl.ds(pl.multiple_of(ROWS - i * CHUNK - (j + 1) * width, 8), width)
                below = u[rows] + c[rows] * below
                u[rows] = below
            return below

        lax.fori_loop(0, CHUNKS, down, zero)
        lax.fori_loop(0, CHUNKS, up, zero)

    per_component(component)


def finish_kernel(got1, got2, got3, u, g, out, wide, buf, sems):
    arrived = [got1[field] + got2[field] + got3[field] for field in range(COUPLED)]

    def copy(i):
        rows = pl.ds(pl.multiple_of(i * CHUNK, CHUNK), CHUNK)
        return pltpu.make_async_copy(buf.at[rows], out.at[rows], sems.at[i])

    def component(levels, tracers):
        width = BLK * tracers
        spread(arrived, tracers, wide)

        def chunk(i, carry):
            b = wide[:width]
            for j in range(CHUNK // width):
                rows = pl.ds(pl.multiple_of(i * CHUNK + j * width, 8), width)
                buf[rows] = u[rows] + b * g[rows]
            copy(i).start()
            return carry

        lax.fori_loop(0, CHUNKS, chunk, 0)

    per_component(component)
    for i in range(CHUNKS):
        copy(i).wait()


def routes(secs, cols):
    every = [(s, c) for s in range(secs) for c in range(cols)]

    def table(move):
        result = []
        for s, c in every:
            to_s, to_c = move(s, c)
            result.append((s * cols + c, (to_s % secs) * cols + to_c % cols))
        return result

    near = table(lambda s, c: (s, c ^ 1))
    far = table(lambda s, c: (s, c + 1 if c % 2 else c - 1))
    turns = [table(lambda s, c, k=k: (s + k, c)) for k in range(1, secs)]
    return near, far, turns


def exchange(own, near, far, tables, work):
    to_near, to_far, turns = tables
    from_far = lax.ppermute(far, AXES, to_far)
    from_near = lax.ppermute(near, AXES, to_near)
    done = work()
    own, *done = lax.optimization_barrier((own, *done))
    total = own + from_near + from_far
    got = [
        lax.ppermute(total[k * COUPLED : (k + 1) * COUPLED], AXES, turns[k])
        for k in range(ROTATIONS)
    ]
    return got, done


def shards(column_state, mixing, surface_mask, pairings, pairing_count, remap_weights):
    tables = routes(lax.axis_size("sec"), lax.axis_size("col"))
    state = column_state[0]
    rates = mixing[0]
    listing = jnp.transpose(pairings, (2, 0, 1))
    points = ROWS * CELLS
    full = ((ROWS, CELLS), f32)
    payload = ((ROTATIONS * COUPLED, BLK, CELLS), f32)
    face = ((COUPLED, BLK, CELLS), f32)
    stack = ((PAIRS * 2 * CELLS, 2 * CELLS), bf16)
    table = ((GOALS, 2 * WBLK * BLK), bf16)
    surface = pltpu.VMEM((WIDE, CELLS), f32)
    products = pltpu.VMEM((COUPLED, WBLK * BLK, CELLS), f32)
    wide = pltpu.VMEM((TAIL, CELLS), f32)

    own, near, far, stacked, counts, sea = call(
        first_kernel,
        [payload, payload, payload, stack, table, ((BLK, CELLS), f32)],
        [state, surface_mask[0], listing, remap_weights[0], pairing_count],
        4,
        [
            pltpu.VMEM((TAIL, CELLS), f32),
            pltpu.VMEM((BLK, CELLS), jnp.int32),
            pltpu.VMEM(listing.shape, jnp.int32),
            pltpu.VMEM((WBLK * CELLS, CELLS), f32),
            surface,
            products,
            pltpu.SemaphoreType.DMA((3,)),
            pltpu.SemaphoreType.DMA((PAIRS,)),
        ],
        6,
        1 << 28,
        1 << 21,
        in_smem=1,
    )

    def sweeps():
        return call(
            sweep_kernel,
            [full] * 5 + [face] * 2,
            [state, rates, sea],
            2,
            [pltpu.VMEM(*full), pltpu.VMEM(*full), pltpu.VMEM(*full), pltpu.SemaphoreType.DMA((2, FETCHES))],
            10,
            20 * points,
            7 * points * 4,
        )

    got, (c, w, e, y, g, y_top, g_top) = exchange(own, near, far, tables, sweeps)

    boundary, own, near, far = call(
        middle_kernel,
        [face, payload, payload, payload],
        [*got, y_top, g_top, sea, stacked, counts],
        0,
        [surface, products],
        4,
        1 << 28,
        1 << 21,
    )

    def again():
        return call(
            again_kernel, [full], [boundary, y, g, w, e, c], 0, [wide], 2, 6 * points, 9 * points * 4
        )

    got, (u,) = exchange(own, near, far, tables, again)

    (out,) = call(
        finish_kernel,
        [full],
        [*got, u, g],
        0,
        [wide, pltpu.VMEM(*full), pltpu.SemaphoreType.DMA((CHUNKS,))],
        5,
        2 * points,
        3 * points * 4,
        True,
    )
    return out[None]


def solution(mesh):
    placed = (
        P("sec", "col", None),
        P("sec", "col", None),
        P("sec", "col", None),
        P("sec", "col", None),
        P("sec", "col"),
        P("sec", "col", None),
    )
    return jax.shard_map(
        shards, mesh=mesh, in_specs=placed, out_specs=P("sec", "col", None), check_vma=False
    )
```

```python
from functools import partial

import jax
import jax.numpy as jnp
from jax import lax
from jax.experimental import pallas as pl
from jax.experimental.pallas import tpu as pltpu
from jax.sharding import PartitionSpec as P

CELLS = 128
LEV_ATM = 128
LEV_OCN = 80
TRC_ATM = 5
TRC_OCN = 8
COUPLED = 4
BLK = 8
WBLK = 16
PAIRS = WBLK // 2
ROWS = 5120
WIDE = BLK * COUPLED
CHUNK = 320
CHUNKS = ROWS // CHUNK
LOADS = 4
LOAD = ROWS // LOADS
FETCHES = 2
FETCH = WBLK * CELLS // FETCHES
TAIL = 64
SECS = 4
ROTATIONS = SECS - 1
GOALS = 80

f32 = jnp.float32
bf16 = jnp.bfloat16
MIB = 1 << 20

ATM = (LEV_ATM, TRC_ATM)
OCN = (LEV_OCN, TRC_OCN)
AXES = ("sec", "col")


def call(kernel, outs, operands, in_hbm, scratch, limit, flops, nbytes, out_hbm=False, in_smem=0):
    vmem = pl.BlockSpec(memory_space=pltpu.VMEM)
    smem = pl.BlockSpec(memory_space=pltpu.SMEM)
    hbm = pl.BlockSpec(memory_space=pltpu.HBM)
    held = [pltpu.with_memory_space_constraint(x, pltpu.HBM) for x in operands[:in_hbm]]
    return pl.pallas_call(
        kernel,
        out_shape=[jax.ShapeDtypeStruct(shape, kind) for shape, kind in outs],
        in_specs=[hbm] * in_hbm + [vmem] * (len(operands) - in_hbm - in_smem) + [smem] * in_smem,
        out_specs=[hbm if out_hbm else vmem] * len(outs),
        scratch_shapes=scratch,
        compiler_params=pltpu.CompilerParams(vmem_limit_bytes=limit * MIB),
        cost_estimate=pl.CostEstimate(flops=flops, bytes_accessed=nbytes, transcendentals=0),
    )(*held, *operands[in_hbm:])


def per_component(body):
    ocean = lax.axis_index("sec") == SECS - 1
    pl.when(ocean)(partial(body, *OCN))
    pl.when(jnp.logical_not(ocean))(partial(body, *ATM))


def blocks_of(start, field, tracers):
    return pl.ds(start + field, BLK, stride=tracers)


def split(values):
    high = values.astype(bf16)
    return high, (values - high.astype(f32)).astype(bf16)


def doubled(surface):
    high, low = split(surface)
    return jnp.concatenate(
        [jnp.concatenate([high, high], axis=1), jnp.concatenate([low, low], axis=1)], axis=0
    )


def multiply(left, stacked, products, pair):
    both = jnp.dot(left, stacked, preferred_element_type=f32)
    both = both[:WIDE] + both[WIDE:]
    for half in range(2):
        for field in range(COUPLED):
            products[field, pl.ds((2 * pair + half) * BLK, BLK)] = both[
                field * BLK : (field + 1) * BLK, half * CELLS : (half + 1) * CELLS
            ]


def deliver(counts, products, targets):
    for first in range(0, COUPLED, 2):
        parts = [split(products[field]) for field in (first, first + 1)]
        right = jnp.concatenate(
            [jnp.concatenate([high, low], axis=0) for high, low in parts], axis=1
        )
        sums = jnp.dot(counts, right, preferred_element_type=f32)
        for t, target in enumerate(targets):
            for slot in range(ROTATIONS):
                row = (t * ROTATIONS + slot) * BLK
                for j in range(2):
                    target[slot * COUPLED + first + j] = sums[
                        row : row + BLK, j * CELLS : (j + 1) * CELLS
                    ]


def count_entries(listing, used):
    columns = lax.axis_size("col")
    sec = lax.axis_index("sec")
    col = lax.axis_index("col")
    source, goal, weight = listing[0], listing[1], listing[2]
    entries = goal.shape[1]
    device = lax.shift_right_logical(goal, BLK.bit_length() - 1)
    to_col = jnp.bitwise_and(device, columns - 1)
    to_sec = lax.shift_right_logical(device, columns.bit_length() - 1)
    slot = jnp.bitwise_and(to_sec - sec + (SECS - 1), SECS - 1)
    place = jnp.where(to_col == col, 0, jnp.where(to_col == jnp.bitwise_xor(col, 1), 1, 2))
    row = (place * ROTATIONS + slot) * BLK + jnp.bitwise_and(goal, BLK - 1)
    position = lax.broadcasted_iota(jnp.int32, (1, entries), 1)
    row = jnp.where(position < used, row, -1)
    combination = weight * BLK + jnp.bitwise_and(source, BLK - 1)
    goals = lax.broadcasted_iota(jnp.int32, (GOALS, entries), 0) == row
    combinations = lax.broadcasted_iota(jnp.int32, (WBLK * BLK, entries), 0) == combination
    counts = lax.dot_general(
        goals.astype(f32).astype(bf16),
        combinations.astype(f32).astype(bf16),
        (((1,), (1,)), ((), ())),
        preferred_element_type=f32,
    ).astype(bf16)
    return jnp.concatenate([counts, counts], axis=1)


def first_kernel(
    state, mask, listing, weights, count, own, near, far, stacked, counts, sea,
    tail, mask_buf, list_buf, w_buf, surface, products, sems, w_sems,
):
    small = [
        pltpu.make_async_copy(listing, list_buf, sems.at[0]),
        pltpu.make_async_copy(state.at[pl.ds(ROWS - TAIL, TAIL)], tail, sems.at[1]),
        pltpu.make_async_copy(mask, mask_buf, sems.at[2]),
    ]
    for copy in small:
        copy.start()

    def fetch(i):
        rows = pl.ds(i * FETCH, FETCH)
        return pltpu.make_async_copy(weights.at[rows], w_buf.at[rows], w_sems.at[i])

    for i in range(FETCHES):
        fetch(i).start()
    for copy in small:
        copy.wait()
    counts[...] = count_entries(list_buf[...], count[0, 0])
    cells = mask_buf[...].astype(f32)
    sea[...] = cells

    def component(levels, tracers):
        for field in range(COUPLED):
            surface[field * BLK : (field + 1) * BLK] = (
                tail[blocks_of(TAIL - BLK * tracers, field, tracers)] * cells
            )

    per_component(component)
    left = doubled(surface[...])
    for p in range(PAIRS):
        base = p * 2 * CELLS
        if base % FETCH == 0:
            fetch(base // FETCH).wait()
        high0, low0 = split(w_buf[base : base + CELLS])
        high1, low1 = split(w_buf[base + CELLS : base + 2 * CELLS])
        both = jnp.concatenate(
            [jnp.concatenate([high0, high1], axis=1), jnp.concatenate([low0, low1], axis=1)], axis=0
        )
        stacked[base : base + 2 * CELLS] = both
        multiply(left, both, products, p)
    deliver(counts[...], products, (own, near, far))


def middle_kernel(
    got1, got2, got3, d_top, c_top, sea, stacked, counts, boundary, own, near, far, surface, products
):
    for field in range(COUPLED):
        arrived = got1[field] + got2[field] + got3[field]
        boundary[field] = arrived
        surface[field * BLK : (field + 1) * BLK] = (
            d_top[field] + c_top[field] * arrived
        ) * sea[...]
    left = doubled(surface[...])
    for p in range(PAIRS):
        base = p * 2 * CELLS
        multiply(left, stacked[base : base + 2 * CELLS], products, p)
    deliver(counts[...], products, (own, near, far))


def spread(values, tracers, wide):
    wide[...] = jnp.zeros_like(wide)
    for field in range(COUPLED):
        wide[blocks_of(0, field, tracers)] = values[field]


def eliminate_kernel(state, mixing, sea, c, w, e, d, c_top, d_top, s_buf, r_buf, sems):
    def copies(i):
        rows = pl.ds(pl.multiple_of(i * LOAD, LOAD), LOAD)
        return (
            pltpu.make_async_copy(mixing.at[rows], r_buf.at[rows], sems.at[0, i]),
            pltpu.make_async_copy(state.at[rows], s_buf.at[rows], sems.at[1, i]),
        )

    for i in range(LOADS):
        for copy in copies(i):
            copy.start()

    def component(levels, tracers):
        width = BLK * tracers
        zero = jnp.zeros((width, CELLS), f32)

        def chunk(i, carry):
            @pl.when(lax.rem(i, LOAD // CHUNK) == 0)
            def _():
                for copy in copies(lax.div(i, LOAD // CHUNK)):
                    copy.wait()

            @pl.when(i == CHUNKS - 1)
            def _():
                for field in range(tracers):
                    r_buf[blocks_of(ROWS - width, field, tracers)] *= sea[...]

            r_above, c_above, d_above = carry
            for j in range(CHUNK // width):
                rows = pl.ds(pl.multiple_of(i * CHUNK + j * width, 8), width)
                r = r_buf[rows]
                inverse = 1.0 / (1.0 + r + r_above * (1.0 - c_above))
                lower = r_above * inverse
                c_above = r * inverse
                d_above = s_buf[rows] * inverse + lower * d_above
                w[rows] = inverse
                e[rows] = lower
                c[rows] = c_above
                d[rows] = d_above
                r_above = r
            return r_above, c_above, d_above

        lax.fori_loop(0, CHUNKS, chunk, (zero, zero, zero))
        for field in range(COUPLED):
            rows = blocks_of(ROWS - width, field, tracers)
            c_top[field] = c[rows]
            d_top[field] = d[rows]

    per_component(component)


def again_kernel(boundary, c, w, e, d, u, g, wide):
    def component(levels, tracers):
        width = BLK * tracers
        per_chunk = CHUNK // width
        spread(boundary, tracers, wide)
        zero = jnp.zeros((width, CELLS), f32)

        def from_end(i, j):
            return pl.ds(pl.multiple_of(ROWS - i * CHUNK - (j + 1) * width, 8), width)

        def first(i, carry):
            x_below, g_below = carry
            for j in range(per_chunk):
                rows = from_end(i, j)
                upper = c[rows]
                x_below = d[rows] + upper * x_below
                g_below = upper * g_below
                u[rows] = x_below
                g[rows] = g_below
            return x_below, g_below

        def down(i, above):
            for j in range(per_chunk):
                rows = pl.ds(pl.multiple_of(i * CHUNK + j * width, 8), width)
                above = u[rows] * w[rows] + e[rows] * above
                u[rows] = above
            return above

        def up(i, below):
            for j in range(per_chunk):
                rows = from_end(i, j)
                below = u[rows] + c[rows] * below
                u[rows] = below
            return below

        lax.fori_loop(0, CHUNKS, first, (wide[:width], jnp.ones_like(zero)))
        lax.fori_loop(0, CHUNKS, down, zero)
        lax.fori_loop(0, CHUNKS, up, zero)

    per_component(component)


def finish_kernel(got1, got2, got3, u, g, out, wide, buf, sems):
    arrived = [got1[field] + got2[field] + got3[field] for field in range(COUPLED)]

    def copy(i):
        rows = pl.ds(pl.multiple_of(i * CHUNK, CHUNK), CHUNK)
        return pltpu.make_async_copy(buf.at[rows], out.at[rows], sems.at[i])

    def component(levels, tracers):
        width = BLK * tracers
        spread(arrived, tracers, wide)

        def chunk(i, carry):
            b = wide[:width]
            for j in range(CHUNK // width):
                rows = pl.ds(pl.multiple_of(i * CHUNK + j * width, 8), width)
                buf[rows] = u[rows] + b * g[rows]
            copy(i).start()
            return carry

        lax.fori_loop(0, CHUNKS, chunk, 0)

    per_component(component)
    for i in range(CHUNKS):
        copy(i).wait()


def routes(secs, cols):
    every = [(s, c) for s in range(secs) for c in range(cols)]

    def table(move):
        result = []
        for s, c in every:
            to_s, to_c = move(s, c)
            result.append((s * cols + c, (to_s % secs) * cols + to_c % cols))
        return result

    near = table(lambda s, c: (s, c ^ 1))
    far = table(lambda s, c: (s, c + 1 if c % 2 else c - 1))
    turns = [table(lambda s, c, k=k: (s + k, c)) for k in range(1, secs)]
    return near, far, turns


def along_col(own, near, far, tables):
    from_near = lax.ppermute(near, AXES, tables[0])
    from_far = lax.ppermute(far, AXES, tables[1])
    return own, from_near, from_far


def along_sec(parts, tables):
    own, from_near, from_far = parts
    total = own + from_near + from_far
    got = [
        lax.ppermute(total[k * COUPLED : (k + 1) * COUPLED], AXES, tables[2][k])
        for k in range(ROTATIONS)
    ]
    return total, got


def shards(column_state, mixing, surface_mask, pairings, pairing_count, remap_weights):
    tables = routes(lax.axis_size("sec"), lax.axis_size("col"))
    state = column_state[0]
    rates = mixing[0]
    listing = jnp.transpose(pairings, (2, 0, 1))
    points = ROWS * CELLS
    full = ((ROWS, CELLS), f32)
    payload = ((ROTATIONS * COUPLED, BLK, CELLS), f32)
    face = ((COUPLED, BLK, CELLS), f32)
    stack = ((PAIRS * 2 * CELLS, 2 * CELLS), bf16)
    table = ((GOALS, 2 * WBLK * BLK), bf16)
    surface = pltpu.VMEM((WIDE, CELLS), f32)
    products = pltpu.VMEM((COUPLED, WBLK * BLK, CELLS), f32)
    wide = pltpu.VMEM((TAIL, CELLS), f32)

    own, near, far, stacked, counts, sea = call(
        first_kernel,
        [payload, payload, payload, stack, table, ((BLK, CELLS), f32)],
        [state, surface_mask[0], listing, remap_weights[0], pairing_count],
        4,
        [
            pltpu.VMEM((TAIL, CELLS), f32),
            pltpu.VMEM((BLK, CELLS), jnp.int32),
            pltpu.VMEM(listing.shape, jnp.int32),
            pltpu.VMEM((WBLK * CELLS, CELLS), f32),
            surface,
            products,
            pltpu.SemaphoreType.DMA((3,)),
            pltpu.SemaphoreType.DMA((FETCHES,)),
        ],
        6,
        1 << 28,
        1 << 21,
        in_smem=1,
    )

    parts = along_col(own, near, far, tables)
    total, got = along_sec(parts, tables)
    total, sea = lax.optimization_barrier((total, sea))
    c, w, e, d, c_top, d_top = call(
        eliminate_kernel,
        [full] * 4 + [face] * 2,
        [state, rates, sea],
        2,
        [pltpu.VMEM(*full), pltpu.VMEM(*full), pltpu.SemaphoreType.DMA((2, LOADS))],
        7,
        20 * points,
        6 * points * 4,
    )
    boundary, own, near, far = call(
        middle_kernel,
        [face, payload, payload, payload],
        [*got, d_top, c_top, sea, stacked, counts],
        0,
        [surface, products],
        4,
        1 << 28,
        1 << 21,
    )

    parts = along_col(own, near, far, tables)
    u, g = call(
        again_kernel, [full] * 2, [boundary, c, w, e, d], 0, [wide], 2, 9 * points, 12 * points * 4
    )
    parts, u, g = lax.optimization_barrier((parts, u, g))
    _, got = along_sec(parts, tables)

    (out,) = call(
        finish_kernel,
        [full],
        [*got, u, g],
        0,
        [wide, pltpu.VMEM(*full), pltpu.SemaphoreType.DMA((CHUNKS,))],
        5,
        2 * points,
        3 * points * 4,
        True,
    )
    return out[None]


def solution(mesh):
    placed = (
        P("sec", "col", None),
        P("sec", "col", None),
        P("sec", "col", None),
        P("sec", "col", None),
        P("sec", "col"),
        P("sec", "col", None),
    )
    return jax.shard_map(
        shards, mesh=mesh, in_specs=placed, out_specs=P("sec", "col", None), check_vma=False
    )
```

```python
from functools import partial

import jax
import jax.numpy as jnp
from jax import lax
from jax.experimental import pallas as pl
from jax.experimental.pallas import tpu as pltpu
from jax.sharding import PartitionSpec as P

CELLS = 128
LEV_ATM = 128
LEV_OCN = 80
TRC_ATM = 5
TRC_OCN = 8
COUPLED = 4
BLK = 8
WBLK = 16
PAIRS = WBLK // 2
ROWS = 5120
WIDE = BLK * COUPLED
CHUNK = 320
CHUNKS = ROWS // CHUNK
LOADS = 4
LOAD = ROWS // LOADS
TAIL = 64
SECS = 4
PARTNERS = SECS - 1
GOALS = 80

f32 = jnp.float32
bf16 = jnp.bfloat16
MIB = 1 << 20

ATM = (LEV_ATM, TRC_ATM)
OCN = (LEV_OCN, TRC_OCN)
AXES = ("sec", "col")


def call(kernel, outs, operands, in_hbm, scratch, limit, flops, nbytes, out_hbm=False, in_smem=0):
    vmem = pl.BlockSpec(memory_space=pltpu.VMEM)
    smem = pl.BlockSpec(memory_space=pltpu.SMEM)
    hbm = pl.BlockSpec(memory_space=pltpu.HBM)
    held = [pltpu.with_memory_space_constraint(x, pltpu.HBM) for x in operands[:in_hbm]]
    return pl.pallas_call(
        kernel,
        out_shape=[jax.ShapeDtypeStruct(shape, kind) for shape, kind in outs],
        in_specs=[hbm] * in_hbm + [vmem] * (len(operands) - in_hbm - in_smem) + [smem] * in_smem,
        out_specs=[hbm if out_hbm else vmem] * len(outs),
        scratch_shapes=scratch,
        compiler_params=pltpu.CompilerParams(vmem_limit_bytes=limit * MIB),
        cost_estimate=pl.CostEstimate(flops=flops, bytes_accessed=nbytes, transcendentals=0),
    )(*held, *operands[in_hbm:])


def per_component(body):
    ocean = lax.axis_index("sec") == SECS - 1
    pl.when(ocean)(partial(body, *OCN))
    pl.when(jnp.logical_not(ocean))(partial(body, *ATM))


def blocks_of(start, field, tracers):
    return pl.ds(start + field, BLK, stride=tracers)


def split(values):
    high = values.astype(bf16)
    return high, (values - high.astype(f32)).astype(bf16)


def doubled(surface):
    high, low = split(surface)
    return jnp.concatenate(
        [jnp.concatenate([high, high], axis=1), jnp.concatenate([low, low], axis=1)], axis=0
    )


def multiply(left, stacked, products, pair):
    both = jnp.dot(left, stacked, preferred_element_type=f32)
    both = both[:WIDE] + both[WIDE:]
    for half in range(2):
        for field in range(COUPLED):
            products[field, pl.ds((2 * pair + half) * BLK, BLK)] = both[
                field * BLK : (field + 1) * BLK, half * CELLS : (half + 1) * CELLS
            ]


def deliver(counts, products, targets):
    for first in range(0, COUPLED, 2):
        parts = [split(products[field]) for field in (first, first + 1)]
        right = jnp.concatenate(
            [jnp.concatenate([high, low], axis=0) for high, low in parts], axis=1
        )
        sums = jnp.dot(counts, right, preferred_element_type=f32)
        for t, target in enumerate(targets):
            for slot in range(PARTNERS):
                row = (t * PARTNERS + slot) * BLK
                for j in range(2):
                    target[slot * COUPLED + first + j] = sums[
                        row : row + BLK, j * CELLS : (j + 1) * CELLS
                    ]


def count_entries(listing, used):
    columns = lax.axis_size("col")
    sec = lax.axis_index("sec")
    col = lax.axis_index("col")
    source, goal, weight = listing[0], listing[1], listing[2]
    entries = goal.shape[1]
    device = lax.shift_right_logical(goal, BLK.bit_length() - 1)
    to_col = jnp.bitwise_and(device, columns - 1)
    to_sec = lax.shift_right_logical(device, columns.bit_length() - 1)
    slot = jnp.where(sec == SECS - 1, to_sec, jnp.full_like(to_sec, sec))
    place = jnp.where(to_col == col, 0, jnp.where(to_col == jnp.bitwise_xor(col, 1), 1, 2))
    row = (place * PARTNERS + slot) * BLK + jnp.bitwise_and(goal, BLK - 1)
    position = lax.broadcasted_iota(jnp.int32, (1, entries), 1)
    row = jnp.where(position < used, row, -1)
    combination = weight * BLK + jnp.bitwise_and(source, BLK - 1)
    goals = lax.broadcasted_iota(jnp.int32, (GOALS, entries), 0) == row
    combinations = lax.broadcasted_iota(jnp.int32, (WBLK * BLK, entries), 0) == combination
    counts = lax.dot_general(
        goals.astype(f32).astype(bf16),
        combinations.astype(f32).astype(bf16),
        (((1,), (1,)), ((), ())),
        preferred_element_type=f32,
    ).astype(bf16)
    return jnp.concatenate([counts, counts], axis=1)


def setup_kernel(state, mask, listing, count, left, counts, sea, tail, mask_buf, list_buf, surface, sems):
    copies = [
        pltpu.make_async_copy(listing, list_buf, sems.at[0]),
        pltpu.make_async_copy(mask, mask_buf, sems.at[1]),
        pltpu.make_async_copy(state.at[pl.ds(ROWS - TAIL, TAIL)], tail, sems.at[2]),
    ]
    for copy in copies:
        copy.start()
    for copy in copies:
        copy.wait()
    counts[...] = count_entries(list_buf[...], count[0, 0])
    cells = mask_buf[...].astype(f32)
    sea[...] = cells

    def component(levels, tracers):
        for field in range(COUPLED):
            surface[field * BLK : (field + 1) * BLK] = (
                tail[blocks_of(TAIL - BLK * tracers, field, tracers)] * cells
            )

    per_component(component)
    left[...] = doubled(surface[...])


def first_kernel(left, counts, weights, own, near, far, stacked, products):
    for p in range(PAIRS):
        base = p * 2 * CELLS
        high0, low0 = split(weights[base : base + CELLS])
        high1, low1 = split(weights[base + CELLS : base + 2 * CELLS])
        both = jnp.concatenate(
            [jnp.concatenate([high0, high1], axis=1), jnp.concatenate([low0, low1], axis=1)], axis=0
        )
        stacked[base : base + 2 * CELLS] = both
        multiply(left[...], both, products, p)
    deliver(counts[...], products, (own, near, far))


def middle_kernel(
    got1, got2, got3, d_top, c_top, sea, stacked, counts, boundary, own, near, far, surface, products
):
    for field in range(COUPLED):
        arrived = got1[field] + got2[field] + got3[field]
        boundary[field] = arrived
        surface[field * BLK : (field + 1) * BLK] = (
            d_top[field] + c_top[field] * arrived
        ) * sea[...]
    left = doubled(surface[...])
    for p in range(PAIRS):
        base = p * 2 * CELLS
        multiply(left, stacked[base : base + 2 * CELLS], products, p)
    deliver(counts[...], products, (own, near, far))


def spread(values, tracers, wide):
    wide[...] = jnp.zeros_like(wide)
    for field in range(COUPLED):
        wide[blocks_of(0, field, tracers)] = values[field]


def eliminate_kernel(state, mixing, sea, c, w, e, d, c_top, d_top, s_buf, r_buf, sems):
    def copies(i):
        rows = pl.ds(pl.multiple_of(i * LOAD, LOAD), LOAD)
        return (
            pltpu.make_async_copy(mixing.at[rows], r_buf.at[rows], sems.at[0, i]),
            pltpu.make_async_copy(state.at[rows], s_buf.at[rows], sems.at[1, i]),
        )

    for i in range(LOADS):
        for copy in copies(i):
            copy.start()

    def component(levels, tracers):
        width = BLK * tracers
        zero = jnp.zeros((width, CELLS), f32)

        def chunk(i, carry):
            @pl.when(lax.rem(i, LOAD // CHUNK) == 0)
            def _():
                for copy in copies(lax.div(i, LOAD // CHUNK)):
                    copy.wait()

            @pl.when(i == CHUNKS - 1)
            def _():
                for field in range(tracers):
                    r_buf[blocks_of(ROWS - width, field, tracers)] *= sea[...]

            r_above, c_above, d_above = carry
            for j in range(CHUNK // width):
                rows = pl.ds(pl.multiple_of(i * CHUNK + j * width, 8), width)
                r = r_buf[rows]
                inverse = 1.0 / (1.0 + r + r_above * (1.0 - c_above))
                lower = r_above * inverse
                c_above = r * inverse
                d_above = s_buf[rows] * inverse + lower * d_above
                w[rows] = inverse
                e[rows] = lower
                c[rows] = c_above
                d[rows] = d_above
                r_above = r
            return r_above, c_above, d_above

        lax.fori_loop(0, CHUNKS, chunk, (zero, zero, zero))
        for field in range(COUPLED):
            rows = blocks_of(ROWS - width, field, tracers)
            c_top[field] = c[rows]
            d_top[field] = d[rows]

    per_component(component)


def again_kernel(boundary, c, w, e, d, u, g, wide):
    def component(levels, tracers):
        width = BLK * tracers
        per_chunk = CHUNK // width
        spread(boundary, tracers, wide)
        zero = jnp.zeros((width, CELLS), f32)

        def from_end(i, j):
            return pl.ds(pl.multiple_of(ROWS - i * CHUNK - (j + 1) * width, 8), width)

        def first(i, carry):
            x_below, g_below = carry
            for j in range(per_chunk):
                rows = from_end(i, j)
                upper = c[rows]
                x_below = d[rows] + upper * x_below
                g_below = upper * g_below
                u[rows] = x_below
                g[rows] = g_below
            return x_below, g_below

        def down(i, above):
            for j in range(per_chunk):
                rows = pl.ds(pl.multiple_of(i * CHUNK + j * width, 8), width)
                above = u[rows] * w[rows] + e[rows] * above
                u[rows] = above
            return above

        def up(i, below):
            for j in range(per_chunk):
                rows = from_end(i, j)
                below = u[rows] + c[rows] * below
                u[rows] = below
            return below

        lax.fori_loop(0, CHUNKS, first, (wide[:width], jnp.ones_like(zero)))
        lax.fori_loop(0, CHUNKS, down, zero)
        lax.fori_loop(0, CHUNKS, up, zero)

    per_component(component)


def finish_kernel(got1, got2, got3, u, g, out, wide, buf, sems):
    arrived = [got1[field] + got2[field] + got3[field] for field in range(COUPLED)]

    def copy(i):
        rows = pl.ds(pl.multiple_of(i * CHUNK, CHUNK), CHUNK)
        return pltpu.make_async_copy(buf.at[rows], out.at[rows], sems.at[i])

    def component(levels, tracers):
        width = BLK * tracers
        spread(arrived, tracers, wide)

        def chunk(i, carry):
            b = wide[:width]
            for j in range(CHUNK // width):
                rows = pl.ds(pl.multiple_of(i * CHUNK + j * width, 8), width)
                buf[rows] = u[rows] + b * g[rows]
            copy(i).start()
            return carry

        lax.fori_loop(0, CHUNKS, chunk, 0)

    per_component(component)
    for i in range(CHUNKS):
        copy(i).wait()


def routes(secs, cols):
    every = [(s, c) for s in range(secs) for c in range(cols)]

    def table(move):
        result = []
        for s, c in every:
            to_s, to_c = move(s, c)
            result.append((s * cols + c, (to_s % secs) * cols + to_c % cols))
        return result

    near = table(lambda s, c: (s, c ^ 1))
    far = table(lambda s, c: (s, c + 1 if c % 2 else c - 1))
    def swap(a):
        def move(s, c):
            if s == a:
                return secs - 1, c
            if s == secs - 1:
                return a, c
            return s, c ^ 1

        return table(move)

    return near, far, [swap(a) for a in range(PARTNERS)]


def along_col(own, near, far, tables):
    from_near = lax.ppermute(near, AXES, tables[0])
    from_far = lax.ppermute(far, AXES, tables[1])
    return own, from_near, from_far


def along_sec(parts, tables):
    own, from_near, from_far = parts
    total = own + from_near + from_far
    got = [
        lax.ppermute(total[k * COUPLED : (k + 1) * COUPLED], AXES, tables[2][k])
        for k in range(PARTNERS)
    ]
    return total, got


def shards(column_state, mixing, surface_mask, pairings, pairing_count, remap_weights):
    tables = routes(lax.axis_size("sec"), lax.axis_size("col"))
    state = column_state[0]
    rates = mixing[0]
    listing = jnp.transpose(pairings, (2, 0, 1))
    points = ROWS * CELLS
    full = ((ROWS, CELLS), f32)
    payload = ((PARTNERS * COUPLED, BLK, CELLS), f32)
    face = ((COUPLED, BLK, CELLS), f32)
    stack = ((PAIRS * 2 * CELLS, 2 * CELLS), bf16)
    table = ((GOALS, 2 * WBLK * BLK), bf16)
    surface = pltpu.VMEM((WIDE, CELLS), f32)
    products = pltpu.VMEM((COUPLED, WBLK * BLK, CELLS), f32)
    wide = pltpu.VMEM((TAIL, CELLS), f32)

    left, counts, sea = call(
        setup_kernel,
        [((2 * WIDE, 2 * CELLS), bf16), table, ((BLK, CELLS), f32)],
        [state, surface_mask[0], listing, pairing_count],
        3,
        [
            pltpu.VMEM((TAIL, CELLS), f32),
            pltpu.VMEM((BLK, CELLS), jnp.int32),
            pltpu.VMEM(listing.shape, jnp.int32),
            surface,
            pltpu.SemaphoreType.DMA((3,)),
        ],
        2,
        1 << 24,
        1 << 17,
        in_smem=1,
    )
    own, near, far, stacked = call(
        first_kernel,
        [payload, payload, payload, stack],
        [left, counts, remap_weights[0]],
        0,
        [products],
        4,
        1 << 28,
        1 << 21,
    )

    parts = along_col(own, near, far, tables)
    total, got = along_sec(parts, tables)
    total, sea = lax.optimization_barrier((total, sea))
    c, w, e, d, c_top, d_top = call(
        eliminate_kernel,
        [full] * 4 + [face] * 2,
        [state, rates, sea],
        2,
        [pltpu.VMEM(*full), pltpu.VMEM(*full), pltpu.SemaphoreType.DMA((2, LOADS))],
        7,
        20 * points,
        6 * points * 4,
    )
    boundary, own, near, far = call(
        middle_kernel,
        [face, payload, payload, payload],
        [*got, d_top, c_top, sea, stacked, counts],
        0,
        [surface, products],
        4,
        1 << 28,
        1 << 21,
    )

    parts = along_col(own, near, far, tables)
    u, g = call(
        again_kernel, [full] * 2, [boundary, c, w, e, d], 0, [wide], 2, 9 * points, 12 * points * 4
    )
    parts, u, g = lax.optimization_barrier((parts, u, g))
    _, got = along_sec(parts, tables)

    (out,) = call(
        finish_kernel,
        [full],
        [*got, u, g],
        0,
        [wide, pltpu.VMEM(*full), pltpu.SemaphoreType.DMA((CHUNKS,))],
        5,
        2 * points,
        3 * points * 4,
        True,
    )
    return out[None]


def solution(mesh):
    placed = (
        P("sec", "col", None),
        P("sec", "col", None),
        P("sec", "col", None),
        P("sec", "col", None),
        P("sec", "col"),
        P("sec", "col", None),
    )
    return jax.shard_map(
        shards, mesh=mesh, in_specs=placed, out_specs=P("sec", "col", None), check_vma=False
    )
```
